32 devices in a mesh: dp: 2 (over core), fsdp: 16 (over z, y, x).
Axes of the slice: x: 2, y: 2, z: 4, core: 2. Of those that a mesh axis runs over, the one named last changes fastest.
Arguments:
- images_in: bfloat16 [32, 22, 22, 768], P(('dp', 'fsdp')), may hold values from -6 to 6
- cotangent: bfloat16 [32, 22, 22, 768], P(('dp', 'fsdp')), may hold values from -6 to 6
- master: float32 [55936, 128], P('fsdp'), may hold values from -2 to 2
- moment: float32 [55936, 128], P('fsdp'), may hold values from -384 to 384
- second: float32 [55936, 128], P('fsdp'), may hold values from 774.4 to 30976
- owner: int32 [37212], replicated, may hold values from 0 to 15, as said below
- offset: int32 [37212], replicated, may hold values from 0 to 3495
Outputs:
- input_grad: bfloat16 [32, 22, 22, 768], P(('dp', 'fsdp'))
- new_master: float32 [55936, 128], P('fsdp')
- new_moment: float32 [55936, 128], P('fsdp')
- new_second: float32 [55936, 128], P('fsdp')
The draws below stay inside these ranges and needn't reach their ends.
Inputs may be any that keep to these rules, and one draw needn't show every extreme that they name: Distinct rows r give distinct slots owner[r] * 3496 + offset[r]. The rows of one owner form one run of consecutive rows, with offsets 0, 1, 2 and so on along it; every owner holds at least one row, and one owner holds exactly 3496.
All inputs are finite; a program needn't handle non-finite values.
Results may differ from the reference program's by a relative error of at most 0.0055.
Values may be sent and summed in bfloat16 or wider, within the bound.
No kernel may reach another device: no remote copies, remote signals or barrier semaphores. Data moves between devices by JAX's collectives and lax.ppermute only.
A program may use at most 128 MiB of HBM per device.

```python
import math
import jax
import jax.numpy as jnp
from jax import lax

C = 768
FF = 3072
KSIZE = 7
SIDE = 22
IMAGES = 32
P_ROWS = 37212
R_DEV = 3496
SLOTS = 55936


def partition(key):
    owners = SLOTS // R_DEV
    order = jax.random.permutation(jax.random.fold_in(key, 11), owners)
    heavy = jax.random.randint(jax.random.fold_in(key, 12), (), 0, owners)
    weights = jax.random.randint(jax.random.fold_in(key, 13), (owners,), 2, 4)
    position = jnp.arange(owners)
    weights = jnp.where(position == heavy, 0, weights)
    running = jnp.cumsum(weights)
    remain = P_ROWS - R_DEV
    bounds = remain * running // running[-1]
    counts = bounds - jnp.concatenate([jnp.zeros((1,), bounds.dtype), bounds[:-1]])
    counts = jnp.where(position == heavy, R_DEV, counts)
    starts = jnp.cumsum(counts) - counts
    flat_rows = jnp.arange(P_ROWS)
    segment = jnp.sum((flat_rows[:, None] >= starts[None, 1:]).astype(jnp.int32), 1)
    owner = order[segment]
    offset = flat_rows - starts[segment]
    return (owner.astype(jnp.int32), offset.astype(jnp.int32))


def draw_owner(key, part):
    return partition(key)[0]


def draw_offset(key, part):
    return partition(key)[1]


def draw_master(key, part):
    owner, offset = partition(key)
    total = P_ROWS * 128
    base = jax.random.truncated_normal(jax.random.fold_in(key, 21), -4.0, 4.0, (total,), jnp.float32)
    level = jax.random.uniform(jax.random.fold_in(key, 22), (total,), jnp.float32, 0.0, 1.0)
    lengths = [KSIZE * KSIZE * C, C, C, C, C * FF, FF, FF * C, C, C]
    edges = []
    running = 0
    for length in lengths[:-1]:
        running = running + length
        edges.append(running)
    position = jnp.arange(total)
    segment = jnp.zeros((total,), jnp.int32)
    for edge in edges:
        segment = segment + (position >= edge).astype(jnp.int32)
    choices_list = [0.2 * base, 0.5 * base, 0.6 + 0.8 * level, 0.3 * base, base * C ** (-0.5), 0.5 * base, base * FF ** (-0.5), 0.3 * base, 0.3 + 0.7 * level]
    values = jnp.zeros((total,), jnp.float32)
    for number, candidate in enumerate(choices_list):
        values = jnp.where(segment == number, candidate, values)
    filler = 0.1 * jax.random.truncated_normal(jax.random.fold_in(key, 23), -4.0, 4.0, (SLOTS, 128), jnp.float32)
    return filler.at[owner * R_DEV + offset].set(values.reshape(P_ROWS, 128))


def block_levels(stream_key, shape, cuts, low, high):
    loudness = 1.0
    for axis_at, parts in cuts:
        heights = jax.random.uniform(jax.random.fold_in(jax.random.fold_in(stream_key, 6), axis_at), (parts,), jnp.float32, low / len(cuts), high / len(cuts))
        loudness = loudness * jnp.repeat(jnp.exp(heights), shape[axis_at] // parts).reshape((-1,) + (1,) * (len(shape) - 1 - axis_at))
    return loudness


def scatter_about(own_key, dims, scale, most, cuts=(), kind=jnp.bfloat16):
    values = scale * jax.random.normal(own_key, dims, jnp.float32)
    if cuts:
        values = values * block_levels(own_key, dims, cuts, -0.22, 0.18)
    return jnp.clip(values, -most, most).astype(kind)


def setup_inputs(seed: int = 0) -> dict:
    key_of = jax.random.split(jax.random.key(seed), 8)
    return {
        "images_in": scatter_about(key_of[0], (IMAGES, SIDE, SIDE, C), 1.0, 6.0, ((0, 32),)),
        "cotangent": scatter_about(key_of[1], (IMAGES, SIDE, SIDE, C), 1.0, 6.0, ((0, 32),)),
        "master": draw_master(jax.random.fold_in(key_of[7], 71), 0),
        "moment": scatter_about(key_of[3], (SLOTS, 128), (0.5 * (IMAGES * SIDE * SIDE) ** 0.5), 384.0, ((0, 16),), jnp.float32),
        "second": jnp.clip(jnp.exp(math.log(30976.0) - 3.6888794 * jax.random.uniform(key_of[4], (SLOTS, 128), jnp.float32) ** block_levels(key_of[4], (SLOTS, 128), ((0, 16),), -0.2, 0.2)), 774.4, 30976.0),
        "owner": draw_owner(jax.random.fold_in(key_of[7], 71), 0),
        "offset": draw_offset(jax.random.fold_in(key_of[7], 71), 0),
    }


ROOT_HALF = 0.7071067811865476
DENSITY = 0.3989422804014327
LEARNING = 0.001
DECAY = 0.05
BETA_ONE = 0.9
BETA_TWO = 0.95
FIRST_FIX = 0.9999734386011124
SECOND_FIX = 0.994079470779666

def split_params(flat, widths, hidden, kernel):
    values = flat.reshape(-1)
    shapes = [(kernel, kernel, widths), (widths,), (widths,), (widths,), (widths, hidden), (hidden,), (hidden, widths), (widths,), (widths,)]
    pieces = []
    start = 0
    for shape in shapes:
        count = math.prod(shape)
        pieces.append(values[start:start + count].reshape(shape))
        start = start + count
    return pieces

def conv_norm(window, depth_kernel, depth_bias, norm_gain, norm_shift):
    reach = depth_kernel.shape[0] // 2
    kernel = depth_kernel.reshape(depth_kernel.shape[0], depth_kernel.shape[1], 1, depth_kernel.shape[2])
    mixed = lax.conv_general_dilated(window[None], kernel, (1, 1), ((0, 0), (reach, reach)), dimension_numbers=('NHWC', 'HWIO', 'NHWC'), feature_group_count=window.shape[-1], precision=lax.Precision.HIGHEST)[0] + depth_bias
    centre = lax.optimization_barrier(jnp.mean(mixed, -1, keepdims=True))
    centred = mixed - centre
    spread = lax.optimization_barrier(jnp.mean(centred * centred, -1, keepdims=True))
    return centred * lax.rsqrt(spread + 1e-06) * norm_gain + norm_shift

def image_pass(window, cot_image, params):
    depth_kernel, depth_bias, norm_gain, norm_shift, weight_in, bias_in, weight_out, bias_out, layer_scale = params
    single = jnp.float32
    widths = window.shape[-1]
    normed, pullback = jax.vjp(conv_norm, window.astype(single), depth_kernel.astype(single), depth_bias.astype(single), norm_gain.astype(single), norm_shift.astype(single))
    normed_low = normed.astype(jnp.bfloat16).reshape(-1, widths)
    before = jnp.dot(normed_low, weight_in, preferred_element_type=single) + bias_in.astype(single)
    activated = (before * 0.5 * (1.0 + lax.erf(before * ROOT_HALF))).astype(jnp.bfloat16)
    branch = jnp.dot(activated, weight_out, preferred_element_type=single) + bias_out.astype(single)
    cot_flat = cot_image.reshape(-1, widths).astype(single)
    branch_grad = (layer_scale.astype(single) * cot_flat).astype(jnp.bfloat16)
    grad_scale = lax.optimization_barrier(jnp.sum(cot_flat * branch, 0))
    grad_bias_out = lax.optimization_barrier(jnp.sum(branch_grad.astype(single), 0))
    grad_weight_out = lax.dot_general(activated, branch_grad, (((0,), (0,)), ((), ())), preferred_element_type=single)
    activated_grad = lax.dot_general(branch_grad, weight_out, (((1,), (1,)), ((), ())), preferred_element_type=single)
    slope = 0.5 * (1.0 + lax.erf(before * ROOT_HALF)) + before * jnp.exp(-0.5 * before * before) * DENSITY
    before_grad = (activated_grad * slope).astype(jnp.bfloat16)
    grad_bias_in = lax.optimization_barrier(jnp.sum(before_grad.astype(single), 0))
    grad_weight_in = lax.dot_general(normed_low, before_grad, (((0,), (0,)), ((), ())), preferred_element_type=single)
    normed_grad = lax.dot_general(before_grad, weight_in, (((1,), (1,)), ((), ())), preferred_element_type=single)
    window_grad, grad_kernel, grad_bias, grad_gain, grad_shift = pullback(normed_grad.reshape(normed.shape))
    lower = jnp.bfloat16
    small_term = jnp.concatenate([grad_kernel.reshape(-1).astype(lower), grad_bias.astype(lower), grad_gain.astype(lower), grad_shift.astype(lower)]).reshape(-1, 128)
    large_term = jnp.concatenate([grad_weight_in.reshape(-1).astype(lower), grad_bias_in.astype(lower), grad_weight_out.reshape(-1).astype(lower), grad_bias_out.astype(lower), grad_scale.astype(lower)]).reshape(-1, 128)
    return (small_term, large_term, window_grad)

def adam_update(gradient, weights, first, second_moment):
    first_new = BETA_ONE * first + (1.0 - BETA_ONE) * gradient
    second_new = BETA_TWO * second_moment + (1.0 - BETA_TWO) * gradient * gradient
    update = first_new / FIRST_FIX / (jnp.sqrt(second_new / SECOND_FIX) + 1e-08)
    weights_new = weights * (1.0 - LEARNING * DECAY) - LEARNING * update
    return (weights_new, first_new, second_new)

def reference(images_in, cotangent, master, moment, second, owner, offset):
    place = (owner * R_DEV + offset).astype(jnp.int32)
    flat = jnp.take(master.astype(jnp.bfloat16), place, axis=0)
    params = split_params(flat, C, FF, KSIZE)
    reach = KSIZE // 2

    def one_image(total, pair):
        picture, cot_picture = pair
        blank = jnp.zeros((reach, SIDE, C), jnp.bfloat16)
        padded = jnp.concatenate([blank, picture, blank], 0)
        small_term, large_term, window_grad = image_pass(padded, cot_picture, params)
        total = total + jnp.concatenate([small_term, large_term], 0).astype(jnp.float32)
        image_grad = (cot_picture.astype(jnp.float32) + window_grad[reach:reach + SIDE]).astype(jnp.bfloat16)
        return (total, image_grad)
    total, image_grads = lax.scan(one_image, jnp.zeros((P_ROWS, 128), jnp.float32), (images_in, cotangent))
    gradient = jnp.zeros((SLOTS, 128), jnp.float32).at[place].set(total)
    new_master, new_moment, new_second = adam_update(gradient, master, moment, second)
    return (image_grads, new_master, new_moment, new_second)
```

```python
import functools

import jax
import jax.numpy as jnp
from jax import lax
from jax.experimental import pallas as pl
from jax.experimental.pallas import tpu as pltpu
from jax.sharding import PartitionSpec as P

C = 768
FF = 3072
KSIZE = 7
TAPS = KSIZE * KSIZE
REACH = KSIZE // 2
SIDE = 22
WIDE = 24

LANES = 128
C_ROWS = C // LANES
FF_ROWS = FF // LANES
HEAD = TAPS + 3
IN_AT = HEAD * C_ROWS
BIN_AT = IN_AT + C * FF_ROWS
OUT_AT = BIN_AT + FF_ROWS
TAIL_AT = OUT_AT + FF * C_ROWS
P_ROWS = TAIL_AT + 2 * C_ROWS
SMALL = 64
STEPS = 6
IN_COLS = FF // STEPS
OUT_ROWS = FF // STEPS
CHUNK = 160
MARGIN = 4096

ROOT_HALF = 0.7071067811865476
DENSITY = 0.3989422804014327
LEARNING = 0.001
DECAY = 0.05
BETA_ONE = 0.9
BETA_TWO = 0.95
FIRST_FIX = 0.9999734386011124
SECOND_FIX = 0.994079470779666

F32 = jnp.float32
BF16 = jnp.bfloat16


def shift_copies(source, padded, shifts, lanes):
    padded[REACH : REACH + SIDE, 8 : 8 + WIDE, :] = source[:, :, lanes].astype(F32)
    for b in range(KSIZE):
        shifts[b] = padded[:, 8 - REACH + b : 8 - REACH + b + WIDE, :]


def lane_block(block):
    return pl.ds(pl.multiple_of(block * LANES, LANES), LANES)


def mix_body(image, small, normed, scaled, inverse, padded, shifts, mixed):
    padded[...] = jnp.zeros_like(padded)

    def channels(block, carry):
        lanes = lane_block(block)
        shift_copies(image, padded, shifts, lanes)

        def rows(group, carry):
            at = group * 11
            total = jnp.broadcast_to(small[TAPS : TAPS + 1, lanes][None], (11, WIDE, LANES))
            for a in range(KSIZE):
                for b in range(KSIZE):
                    tap = small[a * KSIZE + b : a * KSIZE + b + 1, lanes]
                    total = total + tap[None] * shifts[b, pl.ds(at + a, 11)]
            mixed[pl.ds(at, 11), :, lanes] = total
            return carry

        return lax.fori_loop(0, SIDE // 11, rows, carry)

    lax.fori_loop(0, C_ROWS, channels, 0)

    def norm(row, carry):
        value = mixed[row]
        centred = value - jnp.mean(value, -1, keepdims=True)
        spread = jnp.mean(centred * centred, -1, keepdims=True)
        inv = lax.rsqrt(spread + 1e-06)
        unit = centred * inv
        scaled[row] = unit
        inverse[row] = jnp.broadcast_to(inv, (WIDE, LANES))
        normed[row] = (unit * small[TAPS + 1 : TAPS + 2, :] + small[TAPS + 2 : TAPS + 3, :]).astype(BF16)
        return carry

    lax.fori_loop(0, SIDE, norm, 0)


def mix(image, small):
    return pl.pallas_call(
        mix_body,
        out_shape=[
            jax.ShapeDtypeStruct((SIDE, WIDE, C), BF16),
            jax.ShapeDtypeStruct((SIDE, WIDE, C), F32),
            jax.ShapeDtypeStruct((SIDE, WIDE, LANES), F32),
        ],
        scratch_shapes=[
            pltpu.VMEM((SIDE + 2 * REACH, 40, LANES), F32),
            pltpu.VMEM((KSIZE, SIDE + 2 * REACH, WIDE, LANES), F32),
            pltpu.VMEM((SIDE, WIDE, C), F32),
        ],
        name="mix",
    )(image, small)


def unmix_body(
    image, cotangent, small, upstream, scaled, inverse, result, grads, padded, shifts, mixed_grad, taps
):
    padded[...] = jnp.zeros_like(padded)
    grads[...] = jnp.zeros_like(grads)
    gain = small[TAPS + 1 : TAPS + 2, :]

    def fold(value):
        return value[0:8] + value[8:16] + value[16:24]

    def norm(row, carry):
        bias_sum, gain_sum, shift_sum = carry
        up = upstream[row]
        unit = scaled[row]
        inv = inverse[row][:, 0:1]
        scaled_up = up * gain
        first = jnp.mean(scaled_up, -1, keepdims=True)
        second = jnp.mean(scaled_up * unit, -1, keepdims=True)
        value = inv * (scaled_up - first - unit * second)
        mixed_grad[row] = value
        return bias_sum + fold(value), gain_sum + fold(up * unit), shift_sum + fold(up)

    zero = jnp.zeros((8, C), F32)
    sums = lax.fori_loop(0, SIDE, norm, (zero, zero, zero))
    for k in range(3):
        grads[TAPS + k : TAPS + k + 1, :] = jnp.sum(sums[k], 0, keepdims=True)

    def channels(block, carry):
        lanes = lane_block(block)
        shift_copies(mixed_grad, padded, shifts, lanes)
        taps[...] = jnp.zeros_like(taps)

        def rows(group, carry):
            at = group * 2
            source = image[pl.ds(at, 2), :, lanes].astype(F32)
            total = jnp.zeros((2, WIDE, LANES), F32)
            for a in range(KSIZE):
                for b in range(KSIZE):
                    index = TAPS - 1 - (a * KSIZE + b)
                    piece = shifts[b, pl.ds(at + a, 2)]
                    total = total + small[index : index + 1, lanes][None] * piece
                    product = source * piece
                    taps[index] += fold(product[0] + product[1])
            out = cotangent[pl.ds(at, 2), :, lanes].astype(F32) + total
            result[pl.ds(at, 2), :, lanes] = out.astype(BF16)
            return carry

        lax.fori_loop(0, SIDE // 2, rows, 0)
        for index in range(TAPS):
            grads[index : index + 1, lanes] = jnp.sum(taps[index], 0, keepdims=True)
        return carry

    lax.fori_loop(0, C_ROWS, channels, 0)


def unmix(image, cotangent, small, upstream, scaled, inverse):
    return pl.pallas_call(
        unmix_body,
        out_shape=[
            jax.ShapeDtypeStruct((SIDE, WIDE, C), BF16),
            jax.ShapeDtypeStruct((SMALL, C), F32),
        ],
        scratch_shapes=[
            pltpu.VMEM((SIDE + 2 * REACH, 40, LANES), F32),
            pltpu.VMEM((KSIZE, SIDE + 2 * REACH, WIDE, LANES), F32),
            pltpu.VMEM((SIDE, WIDE, C), F32),
            pltpu.VMEM((TAPS, 8, LANES), F32),
        ],
        name="unmix",
    )(image, cotangent, small, upstream, scaled, inverse)


def unpack_body(parts, rows, owners, order, starts, counts, slots, small, w_in, w_out, flat):
    step = pl.program_id(0)

    @pl.when(step < owners)
    def _():
        start = starts[step]
        count = counts[step]
        for part in range(parts):
            left = jnp.clip(count - part * rows, 0, rows)
            trips = (left + CHUNK - 1) // CHUNK

            def copy(k, carry, part=part):
                at = pl.multiple_of(k * CHUNK, 16)
                piece = slots[part, pl.ds(at, CHUNK), :].astype(F32)
                flat[pl.ds(start + part * rows + k * CHUNK, CHUNK), :] = piece
                return carry

            lax.fori_loop(0, trips, copy, 0)

    @pl.when(step == owners)
    def _():
        for j in range(C_ROWS):
            lane = slice(j * LANES, (j + 1) * LANES)
            small[0:HEAD, lane] = flat[pl.ds(j, HEAD, stride=C_ROWS), :]
            small[HEAD : HEAD + 4, lane] = flat[pl.ds(BIN_AT + j, 4, stride=C_ROWS), :]
            small[HEAD + 4 : HEAD + 6, lane] = flat[pl.ds(TAIL_AT + j, 2, stride=C_ROWS), :]

    @pl.when(step >= owners)
    def _():
        block = step - owners
        for j in range(IN_COLS // LANES):
            at = IN_AT + block * (IN_COLS // LANES) + j
            w_in[:, j * LANES : (j + 1) * LANES] = flat[pl.ds(at, C, stride=FF_ROWS), :].astype(BF16)
        for j in range(C_ROWS):
            at = OUT_AT + block * (OUT_ROWS * C_ROWS) + j
            w_out[:, j * LANES : (j + 1) * LANES] = flat[pl.ds(at, OUT_ROWS, stride=C_ROWS), :].astype(BF16)


def unpack(gathered, order, starts, counts):
    parts, span, _ = gathered.shape
    owners = order.shape[0]
    rows = span // owners
    late = lambda i: jnp.maximum(i - owners, 0)
    grid_spec = pltpu.PrefetchScalarGridSpec(
        num_scalar_prefetch=3,
        grid=(owners + STEPS,),
        in_specs=[
            pl.BlockSpec(
                (parts, rows, LANES),
                lambda i, o, s, c: (0, o[jnp.minimum(i, owners - 1)], 0),
            )
        ],
        out_specs=[
            pl.BlockSpec((SMALL, C), lambda i, o, s, c: (0, 0)),
            pl.BlockSpec((C, IN_COLS), lambda i, o, s, c: (0, late(i))),
            pl.BlockSpec((OUT_ROWS, C), lambda i, o, s, c: (late(i), 0)),
        ],
        scratch_shapes=[pltpu.VMEM((P_ROWS + MARGIN, LANES), F32)],
    )
    return pl.pallas_call(
        functools.partial(unpack_body, parts, rows, owners),
        grid_spec=grid_spec,
        out_shape=[
            jax.ShapeDtypeStruct((SMALL, C), F32),
            jax.ShapeDtypeStruct((C, FF), BF16),
            jax.ShapeDtypeStruct((FF, C), BF16),
        ],
        name="unpack",
    )(order, starts, counts, gathered)


def pack_body(paired, groups, owners, bases, *refs):
    inputs = 5 if paired else 3
    small = refs[0]
    in_refs = refs[1:inputs:2] if paired else refs[1:2]
    out_refs = refs[2:inputs:2] if paired else refs[2:3]
    outs = refs[inputs:-1]
    flat = refs[-1]
    step = pl.program_id(0)

    def total(parts, index):
        value = parts[0][index].astype(F32)
        for other in parts[1:]:
            value = value + other[index].astype(F32)
        return value

    @pl.when(step == 0)
    def _():
        for j in range(C_ROWS):
            lane = slice(j * LANES, (j + 1) * LANES)
            flat[pl.ds(j, HEAD, stride=C_ROWS), :] = small[0:HEAD, lane]
            flat[pl.ds(BIN_AT + j, 4, stride=C_ROWS), :] = small[HEAD : HEAD + 4, lane]
            flat[pl.ds(TAIL_AT + j, 2, stride=C_ROWS), :] = small[HEAD + 4 : HEAD + 6, lane]
        flat[P_ROWS : P_ROWS + MARGIN, :] = jnp.zeros((MARGIN, LANES), F32)

    @pl.when(step < STEPS)
    def _():
        for j in range(IN_COLS // LANES):
            at = IN_AT + step * (IN_COLS // LANES) + j
            index = (slice(None), slice(j * LANES, (j + 1) * LANES))
            flat[pl.ds(at, C, stride=FF_ROWS), :] = total(in_refs, index)
        for j in range(C_ROWS):
            at = OUT_AT + step * (OUT_ROWS * C_ROWS) + j
            index = (slice(None), slice(j * LANES, (j + 1) * LANES))
            flat[pl.ds(at, OUT_ROWS, stride=C_ROWS), :] = total(out_refs, index)

    slot = step - STEPS
    for (table, first, count, row, rows), out in zip(groups, outs, strict=True):

        @pl.when((slot >= first) & (slot < first + count))
        def _(table=table, row=row, rows=rows, out=out):
            base = bases[table * owners + slot] + row
            for at in range(0, rows, 16):
                out[0, at : at + 16, :] = flat[pl.ds(base + at, 16), :].astype(BF16)


def pack(bases, small, ins, outs, owners, groups):
    paired = len(ins) == 2
    early = lambda i: jnp.minimum(i, STEPS - 1)
    operands = [small]
    in_specs = [pl.BlockSpec((SMALL, C), lambda i, b: (0, 0))]
    for w_in, w_out in zip(ins, outs, strict=True):
        operands += [w_in, w_out]
        in_specs += [
            pl.BlockSpec((C, IN_COLS), lambda i, b: (0, early(i))),
            pl.BlockSpec((OUT_ROWS, C), lambda i, b: (early(i), 0)),
        ]
    out_specs = [
        pl.BlockSpec(
            (1, rows, LANES),
            lambda i, b, first=first, count=count: (jnp.clip(i - STEPS - first, 0, count - 1), 0, 0),
        )
        for table, first, count, row, rows in groups
    ]
    grid_spec = pltpu.PrefetchScalarGridSpec(
        num_scalar_prefetch=1,
        grid=(STEPS + owners,),
        in_specs=in_specs,
        out_specs=out_specs,
        scratch_shapes=[pltpu.VMEM((P_ROWS + MARGIN, LANES), F32)],
    )
    return pl.pallas_call(
        functools.partial(pack_body, paired, groups, owners),
        grid_spec=grid_spec,
        out_shape=[
            jax.ShapeDtypeStruct((count, rows, LANES), BF16) for table, first, count, row, rows in groups
        ],
        name="pack",
    )(bases, *operands)


def add(*values):
    total = values[0].astype(F32)
    for value in values[1:]:
        total = total + value.astype(F32)
    return total


def swap(value, mask, size):
    return lax.ppermute(value, "fsdp", [(i, i ^ mask) for i in range(size)])


def reduce_part(far, near, home, masks, size):
    got = swap(far, masks[0], size)
    half = near.shape[0]
    near = add(near, got[half:]).astype(BF16)
    back = swap(near, masks[1], size)
    home = add(home, got[:half], back)
    low = home.astype(BF16)
    pieces = [swap(low[k], 4 * k, size) for k in (1, 2, 3)]
    return add(home[0], *pieces).astype(BF16)


def image_pass(image, cot_image, small, weight_in, weight_out):
    bias_in = small[HEAD : HEAD + 4].reshape(-1)
    bias_out, layer_scale = small[HEAD + 4], small[HEAD + 5]
    normed, scaled, inverse = mix(image, small)
    normed_low = normed.reshape(-1, C)
    before = jnp.dot(normed_low, weight_in, preferred_element_type=F32) + bias_in
    activated = (before * 0.5 * (1.0 + lax.erf(before * ROOT_HALF))).astype(BF16)
    branch = jnp.dot(activated, weight_out, preferred_element_type=F32) + bias_out
    cot_flat = cot_image.reshape(-1, C).astype(F32)
    branch_grad = (layer_scale * cot_flat).astype(BF16)
    grad_scale = jnp.sum(cot_flat * branch, 0)
    grad_bias_out = jnp.sum(branch_grad.astype(F32), 0)
    grad_weight_out = lax.dot_general(
        activated, branch_grad, (((0,), (0,)), ((), ())), preferred_element_type=F32
    ).astype(BF16)
    activated_grad = lax.dot_general(
        branch_grad, weight_out, (((1,), (1,)), ((), ())), preferred_element_type=F32
    )
    slope = (
        0.5 * (1.0 + lax.erf(before * ROOT_HALF))
        + before * jnp.exp(-0.5 * before * before) * DENSITY
    )
    before_grad = (activated_grad * slope).astype(BF16)
    grad_bias_in = jnp.sum(before_grad.astype(F32), 0)
    grad_weight_in = lax.dot_general(
        normed_low, before_grad, (((0,), (0,)), ((), ())), preferred_element_type=F32
    ).astype(BF16)
    normed_grad = lax.dot_general(
        before_grad, weight_in, (((1,), (1,)), ((), ())), preferred_element_type=F32
    )
    result, head_grad = unmix(
        image, cot_image, small, normed_grad.reshape(SIDE, WIDE, C), scaled, inverse
    )
    small_grad = jnp.concatenate(
        [
            head_grad[:HEAD],
            grad_bias_in.reshape(-1, C),
            grad_bias_out[None],
            grad_scale[None],
            jnp.zeros((SMALL - HEAD - 6, C), F32),
        ]
    ).astype(BF16)
    return small_grad, grad_weight_in, grad_weight_out, result


def adam_update(gradient, weights, first, second_moment):
    first_new = BETA_ONE * first + (1.0 - BETA_ONE) * gradient
    second_new = BETA_TWO * second_moment + (1.0 - BETA_TWO) * gradient * gradient
    update = first_new / FIRST_FIX / (jnp.sqrt(second_new / SECOND_FIX) + 1e-08)
    weights_new = weights * (1.0 - LEARNING * DECAY) - LEARNING * update
    return (weights_new, first_new, second_new)


def per_device(images_in, cotangent, master, moment, second, owner, offset):
    owners = lax.axis_size("fsdp")
    replicas = lax.axis_size("dp")
    me = lax.axis_index("fsdp")
    core = lax.axis_index("dp")
    bucket = master.shape[0]
    total_rows = owner.shape[0]
    rows = -(-bucket // (replicas * CHUNK)) * CHUNK

    ids = jnp.arange(owners, dtype=jnp.int32)
    positions = jnp.arange(total_rows, dtype=jnp.int32)
    begins = jnp.where(offset == 0, positions, 0)
    starts = jnp.sum(jnp.where(owner[None, :] == ids[:, None], begins[None, :], 0), 1)
    rank = jnp.sum((starts[None, :] < starts[:, None]).astype(jnp.int32), 1)
    later = jnp.where(starts[None, :] > starts[:, None], starts[None, :], total_rows)
    counts = jnp.min(later, 1) - starts
    chosen = rank[None, :] == ids[:, None]
    pick = lambda mask, values: jnp.sum(jnp.where(mask, values[None, :], 0), 1)

    lowered = jnp.pad(master, ((0, replicas * rows - bucket), (0, 0))).astype(BF16)
    mine = lax.dynamic_slice_in_dim(lowered, core * rows, rows, 0)
    gathered = lax.all_gather(mine, ("dp", "fsdp"), axis=0, tiled=True)
    small, weight_in, weight_out = unpack(
        gathered.reshape(replicas, owners * rows, LANES),
        pick(chosen, ids),
        pick(chosen, starts),
        pick(chosen, counts),
    )

    widen = lambda value: jnp.pad(value[0], ((0, 0), (0, WIDE - SIDE), (0, 0)))
    small_grad, grad_in, grad_out, result = image_pass(
        widen(images_in), widen(cotangent), small, weight_in, weight_out
    )
    input_grad = result[None, :, :SIDE]

    if replicas == 2 and owners == 16:
        other = lambda value: lax.ppermute(value, "dp", [(0, 1), (1, 0)])
        far_out, far_in, far_small = other(grad_out), other(grad_in), other(small_grad)
        quarter = rows // 32 * 8 // 16 * 16
        sizes = [quarter, quarter, rows // 2 - quarter, rows // 2 - quarter]
        groups = []
        at = 0
        for number, size in enumerate(sizes):
            groups += [(number % 2, f, c, at, size) for f, c in ((8, 8), (4, 4), (0, 4))]
            at += size
        spots = jnp.arange(16, dtype=jnp.int32)
        high, low, deep = spots >> 3, (spots >> 2) & 1, spots & 3
        tables = [deep * 4 + high * 2 + low, deep * 4 + low * 2 + high]
        bases = jnp.concatenate(
            [pick((table ^ me)[:, None] == ids[None, :], starts) for table in tables]
        ) + core * rows
        packed = pack(
            bases, add(small_grad, far_small), (grad_in, far_in), (grad_out, far_out), owners, groups
        )
        sums = [
            reduce_part(*packed[3 * k : 3 * k + 3], (2, 1) if k % 2 == 0 else (1, 2), owners)
            for k in range(4)
        ]
        half = jnp.concatenate(sums, 0)
        theirs = other(half)
        grad_low = jnp.where(
            core == 0, jnp.concatenate([half, theirs]), jnp.concatenate([theirs, half])
        )
    else:
        groups = [(0, 0, owners, part * rows, rows) for part in range(replicas)]
        packed = pack(starts, small_grad.astype(F32), (grad_in,), (grad_out,), owners, groups)
        stacked = jnp.concatenate([value.reshape(owners * rows, LANES) for value in packed])
        part = lax.psum_scatter(stacked, "dp", scatter_dimension=0, tiled=True)
        half = lax.psum_scatter(part, "fsdp", scatter_dimension=0, tiled=True)
        grad_low = lax.all_gather(half, "dp", axis=0, tiled=True)

    mine_count = jnp.sum(jnp.where(ids == me, counts, 0))
    valid = jnp.arange(bucket)[:, None] < mine_count
    grad_full = jnp.where(valid, grad_low[:bucket].astype(F32), 0.0)
    new_master, new_moment, new_second = adam_update(grad_full, master, moment, second)
    return (input_grad, new_master, new_moment, new_second)


def solution(mesh):
    placed = (
        P(("dp", "fsdp"), None, None, None),
        P(("dp", "fsdp"), None, None, None),
        P("fsdp", None),
        P("fsdp", None),
        P("fsdp", None),
        P(),
        P(),
    )
    return jax.shard_map(
        per_device,
        mesh=mesh,
        in_specs=placed,
        out_specs=(
            P(("dp", "fsdp"), None, None, None),
            P("fsdp", None),
            P("fsdp", None),
            P("fsdp", None),
        ),
        check_vma=False,
    )
```

```python
import functools

import jax
import jax.numpy as jnp
from jax import lax
from jax.experimental import pallas as pl
from jax.experimental.pallas import tpu as pltpu
from jax.sharding import PartitionSpec as P


C = 768
FF = 3072
KSIZE = 7
TAPS = KSIZE * KSIZE
REACH = KSIZE // 2
SIDE = 22
WIDE = 24

LANES = 128
C_ROWS = C // LANES
FF_ROWS = FF // LANES
HEAD = TAPS + 3
IN_AT = HEAD * C_ROWS
BIN_AT = IN_AT + C * FF_ROWS
OUT_AT = BIN_AT + FF_ROWS
TAIL_AT = OUT_AT + FF * C_ROWS
P_ROWS = TAIL_AT + 2 * C_ROWS
SMALL = 8
HEAD_PAD = 56
STEPS = 6
IN_COLS = FF // STEPS
OUT_ROWS = FF // STEPS
CHUNK = 160
MARGIN = 4096

ROOT_HALF = 0.7071067811865476
DENSITY = 0.3989422804014327
LEARNING = 0.001
DECAY = 0.05
BETA_ONE = 0.9
BETA_TWO = 0.95
FIRST_FIX = 0.9999734386011124
SECOND_FIX = 0.994079470779666

F32 = jnp.float32
BF16 = jnp.bfloat16


def shift_copies(source, padded, shifts, lanes):
    padded[REACH : REACH + SIDE, 8 : 8 + WIDE, :] = source[:, :, lanes].astype(F32)
    for b in range(KSIZE):
        shifts[b] = padded[:, 8 - REACH + b : 8 - REACH + b + WIDE, :]


def lane_block(block):
    return pl.ds(pl.multiple_of(block * LANES, LANES), LANES)


def mix_body(image, small, normed, scaled, inverse, padded, shifts, mixed):
    padded[...] = jnp.zeros_like(padded)

    def channels(block, carry):
        lanes = lane_block(block)
        shift_copies(image, padded, shifts, lanes)

        def rows(group, carry):
            at = group * 11
            total = jnp.broadcast_to(small[TAPS : TAPS + 1, lanes][None], (11, WIDE, LANES))
            for a in range(KSIZE):
                for b in range(KSIZE):
                    tap = small[a * KSIZE + b : a * KSIZE + b + 1, lanes]
                    total = total + tap[None] * shifts[b, pl.ds(at + a, 11)]
            mixed[pl.ds(at, 11), :, lanes] = total
            return carry

        return lax.fori_loop(0, SIDE // 11, rows, carry)

    lax.fori_loop(0, C_ROWS, channels, 0)

    def norm(row, carry):
        value = mixed[row]
        centred = value - jnp.mean(value, -1, keepdims=True)
        spread = jnp.mean(centred * centred, -1, keepdims=True)
        inv = lax.rsqrt(spread + 1e-06)
        unit = centred * inv
        scaled[row] = unit
        inverse[row] = jnp.broadcast_to(inv, (WIDE, LANES))
        normed[row] = (unit * small[TAPS + 1 : TAPS + 2, :] + small[TAPS + 2 : TAPS + 3, :]).astype(BF16)
        return carry

    lax.fori_loop(0, SIDE, norm, 0)


def mix(image, small):
    return pl.pallas_call(
        mix_body,
        out_shape=[
            jax.ShapeDtypeStruct((SIDE, WIDE, C), BF16),
            jax.ShapeDtypeStruct((SIDE, WIDE, C), F32),
            jax.ShapeDtypeStruct((SIDE, WIDE, LANES), F32),
        ],
        scratch_shapes=[
            pltpu.VMEM((SIDE + 2 * REACH, 40, LANES), F32),
            pltpu.VMEM((KSIZE, SIDE + 2 * REACH, WIDE, LANES), F32),
            pltpu.VMEM((SIDE, WIDE, C), F32),
        ],
        name="mix",
    )(image, small)


def unmix_body(
    image, cotangent, small, upstream, scaled, inverse, result, grads, padded, shifts, mixed_grad, taps
):
    padded[...] = jnp.zeros_like(padded)
    grads[...] = jnp.zeros_like(grads)
    gain = small[TAPS + 1 : TAPS + 2, :]

    def fold(value):
        return value[0:8] + value[8:16] + value[16:24]

    def norm(row, carry):
        bias_sum, gain_sum, shift_sum = carry
        up = upstream[row]
        unit = scaled[row]
        inv = inverse[row][:, 0:1]
        scaled_up = up * gain
        first = jnp.mean(scaled_up, -1, keepdims=True)
        second = jnp.mean(scaled_up * unit, -1, keepdims=True)
        value = inv * (scaled_up - first - unit * second)
        mixed_grad[row] = value
        return bias_sum + fold(value), gain_sum + fold(up * unit), shift_sum + fold(up)

    zero = jnp.zeros((8, C), F32)
    sums = lax.fori_loop(0, SIDE, norm, (zero, zero, zero))
    for k in range(3):
        grads[TAPS + k : TAPS + k + 1, :] = jnp.sum(sums[k], 0, keepdims=True)

    def channels(block, carry):
        lanes = lane_block(block)
        shift_copies(mixed_grad, padded, shifts, lanes)
        taps[...] = jnp.zeros_like(taps)

        def rows(group, carry):
            at = group * 2
            source = image[pl.ds(at, 2), :, lanes].astype(F32)
            total = jnp.zeros((2, WIDE, LANES), F32)
            for a in range(KSIZE):
                for b in range(KSIZE):
                    index = TAPS - 1 - (a * KSIZE + b)
                    piece = shifts[b, pl.ds(at + a, 2)]
                    total = total + small[index : index + 1, lanes][None] * piece
                    product = source * piece
                    taps[index] += fold(product[0] + product[1])
            out = cotangent[pl.ds(at, 2), :, lanes].astype(F32) + total
            result[pl.ds(at, 2), :, lanes] = out.astype(BF16)
            return carry

        lax.fori_loop(0, SIDE // 2, rows, 0)
        for index in range(TAPS):
            grads[index : index + 1, lanes] = jnp.sum(taps[index], 0, keepdims=True)
        return carry

    lax.fori_loop(0, C_ROWS, channels, 0)


def unmix(image, cotangent, small, upstream, scaled, inverse):
    return pl.pallas_call(
        unmix_body,
        out_shape=[
            jax.ShapeDtypeStruct((SIDE, WIDE, C), BF16),
            jax.ShapeDtypeStruct((HEAD_PAD, C), F32),
        ],
        scratch_shapes=[
            pltpu.VMEM((SIDE + 2 * REACH, 40, LANES), F32),
            pltpu.VMEM((KSIZE, SIDE + 2 * REACH, WIDE, LANES), F32),
            pltpu.VMEM((SIDE, WIDE, C), F32),
            pltpu.VMEM((TAPS, 8, LANES), F32),
        ],
        name="unmix",
    )(image, cotangent, small, upstream, scaled, inverse)


def unpack_body(parts, rows, owners, order, starts, counts, slots, small, w_in, w_out, flat):
    step = pl.program_id(0)

    @pl.when(step < owners)
    def _():
        start = starts[step]
        count = counts[step]
        for part in range(parts):
            left = jnp.clip(count - part * rows, 0, rows)
            trips = (left + CHUNK - 1) // CHUNK

            def copy(k, carry, part=part):
                at = pl.multiple_of(k * CHUNK, 16)
                piece = slots[part, pl.ds(at, CHUNK), :].astype(F32)
                flat[pl.ds(start + part * rows + k * CHUNK, CHUNK), :] = piece
                return carry

            lax.fori_loop(0, trips, copy, 0)

    @pl.when(step == owners)
    def _():
        for j in range(C_ROWS):
            lane = slice(j * LANES, (j + 1) * LANES)
            small[0:4, lane] = flat[pl.ds(BIN_AT + j, 4, stride=C_ROWS), :]
            small[4:6, lane] = flat[pl.ds(TAIL_AT + j, 2, stride=C_ROWS), :]

    @pl.when(step >= owners)
    def _():
        block = step - owners
        for j in range(IN_COLS // LANES):
            at = IN_AT + block * (IN_COLS // LANES) + j
            w_in[:, j * LANES : (j + 1) * LANES] = flat[pl.ds(at, C, stride=FF_ROWS), :].astype(BF16)
        for j in range(C_ROWS):
            at = OUT_AT + block * (OUT_ROWS * C_ROWS) + j
            w_out[:, j * LANES : (j + 1) * LANES] = flat[pl.ds(at, OUT_ROWS, stride=C_ROWS), :].astype(BF16)


def unpack(gathered, order, starts, counts):
    parts, span, _ = gathered.shape
    owners = order.shape[0]
    rows = span // owners
    late = lambda i: jnp.maximum(i - owners, 0)
    grid_spec = pltpu.PrefetchScalarGridSpec(
        num_scalar_prefetch=3,
        grid=(owners + STEPS,),
        in_specs=[
            pl.BlockSpec(
                (parts, rows, LANES),
                lambda i, o, s, c: (0, o[jnp.minimum(i, owners - 1)], 0),
            )
        ],
        out_specs=[
            pl.BlockSpec((SMALL, C), lambda i, o, s, c: (0, 0)),
            pl.BlockSpec((C, IN_COLS), lambda i, o, s, c: (0, late(i))),
            pl.BlockSpec((OUT_ROWS, C), lambda i, o, s, c: (late(i), 0)),
        ],
        scratch_shapes=[pltpu.VMEM((P_ROWS + MARGIN, LANES), F32)],
    )
    return pl.pallas_call(
        functools.partial(unpack_body, parts, rows, owners),
        grid_spec=grid_spec,
        out_shape=[
            jax.ShapeDtypeStruct((SMALL, C), F32),
            jax.ShapeDtypeStruct((C, FF), BF16),
            jax.ShapeDtypeStruct((FF, C), BF16),
        ],
        name="unpack",
    )(order, starts, counts, gathered)


def pack_body(paired, groups, owners, bases, *refs):
    inputs = 5 if paired else 3
    small = refs[0]
    in_refs = refs[1:inputs:2] if paired else refs[1:2]
    out_refs = refs[2:inputs:2] if paired else refs[2:3]
    outs = refs[inputs:-1]
    flat = refs[-1]
    step = pl.program_id(0)

    def total(parts, index):
        value = parts[0][index].astype(F32)
        for other in parts[1:]:
            value = value + other[index].astype(F32)
        return value

    @pl.when(step == 0)
    def _():
        for j in range(C_ROWS):
            lane = slice(j * LANES, (j + 1) * LANES)
            flat[pl.ds(BIN_AT + j, 4, stride=C_ROWS), :] = small[0:4, lane]
            flat[pl.ds(TAIL_AT + j, 2, stride=C_ROWS), :] = small[4:6, lane]
        flat[0:IN_AT, :] = jnp.zeros((IN_AT, LANES), F32)
        flat[P_ROWS : P_ROWS + MARGIN, :] = jnp.zeros((MARGIN, LANES), F32)

    @pl.when(step < STEPS)
    def _():
        for j in range(IN_COLS // LANES):
            at = IN_AT + step * (IN_COLS // LANES) + j
            index = (slice(None), slice(j * LANES, (j + 1) * LANES))
            flat[pl.ds(at, C, stride=FF_ROWS), :] = total(in_refs, index)
        for j in range(C_ROWS):
            at = OUT_AT + step * (OUT_ROWS * C_ROWS) + j
            index = (slice(None), slice(j * LANES, (j + 1) * LANES))
            flat[pl.ds(at, OUT_ROWS, stride=C_ROWS), :] = total(out_refs, index)

    slot = step - STEPS
    for (table, first, count, row, rows), out in zip(groups, outs, strict=True):

        @pl.when((slot >= first) & (slot < first + count))
        def _(table=table, row=row, rows=rows, out=out):
            base = bases[table * owners + slot] + row
            for at in range(0, rows, 16):
                out[0, at : at + 16, :] = flat[pl.ds(base + at, 16), :].astype(BF16)


def pack(bases, small, ins, outs, owners, groups):
    paired = len(ins) == 2
    early = lambda i: jnp.minimum(i, STEPS - 1)
    operands = [small]
    in_specs = [pl.BlockSpec((SMALL, C), lambda i, b: (0, 0))]
    for w_in, w_out in zip(ins, outs, strict=True):
        operands += [w_in, w_out]
        in_specs += [
            pl.BlockSpec((C, IN_COLS), lambda i, b: (0, early(i))),
            pl.BlockSpec((OUT_ROWS, C), lambda i, b: (early(i), 0)),
        ]
    out_specs = [
        pl.BlockSpec(
            (1, rows, LANES),
            lambda i, b, first=first, count=count: (jnp.clip(i - STEPS - first, 0, count - 1), 0, 0),
        )
        for table, first, count, row, rows in groups
    ]
    grid_spec = pltpu.PrefetchScalarGridSpec(
        num_scalar_prefetch=1,
        grid=(STEPS + owners,),
        in_specs=in_specs,
        out_specs=out_specs,
        scratch_shapes=[pltpu.VMEM((P_ROWS + MARGIN, LANES), F32)],
    )
    return pl.pallas_call(
        functools.partial(pack_body, paired, groups, owners),
        grid_spec=grid_spec,
        out_shape=[
            jax.ShapeDtypeStruct((count, rows, LANES), BF16) for table, first, count, row, rows in groups
        ],
        name="pack",
    )(bases, *operands)


def add(*values):
    total = values[0].astype(F32)
    for value in values[1:]:
        total = total + value.astype(F32)
    return total


def swap(value, mask, size):
    return lax.ppermute(value, "fsdp", [(i, i ^ mask) for i in range(size)])


def sum_small(value, size):
    mask = 1
    while mask < size:
        value = add(value, swap(value, mask, size)).astype(BF16)
        mask *= 2
    return value


def replica_others(value, replicas):
    turn = lambda k: [(i, (i + k) % replicas) for i in range(replicas)]
    return [lax.ppermute(value, "dp", turn(k)) for k in range(1, replicas)]


def first_phase(far, near, home, masks, size):
    got = swap(far, masks[0], size)
    half = near.shape[0]
    return add(near, got[half:]).astype(BF16), add(home, got[:half])


def second_phase(near, home, masks, size):
    return home + swap(near, masks[1], size).astype(F32)


def last_phase(home, shift, size):
    low = home.astype(BF16)
    pieces = [swap(low[k], k * shift, size) for k in (1, 2, 3)]
    return add(home[0], *pieces).astype(BF16)


def after(value, gates):
    return lax.optimization_barrier((value, *gates))[0]


def forward_backward(normed, cot_image, small, weight_in, weight_out):
    bias_in = small[0:4].reshape(-1)
    bias_out, layer_scale = small[4], small[5]
    normed_low = normed.reshape(-1, C)
    before = jnp.dot(normed_low, weight_in, preferred_element_type=F32) + bias_in
    activated = (before * 0.5 * (1.0 + lax.erf(before * ROOT_HALF))).astype(BF16)
    branch = jnp.dot(activated, weight_out, preferred_element_type=F32) + bias_out
    cot_flat = cot_image.reshape(-1, C).astype(F32)
    branch_grad = (layer_scale * cot_flat).astype(BF16)
    grad_scale = jnp.sum(cot_flat * branch, 0)
    grad_bias_out = jnp.sum(branch_grad.astype(F32), 0)
    grad_weight_out = lax.dot_general(
        activated, branch_grad, (((0,), (0,)), ((), ())), preferred_element_type=F32
    ).astype(BF16)
    activated_grad = lax.dot_general(
        branch_grad, weight_out, (((1,), (1,)), ((), ())), preferred_element_type=F32
    )
    slope = (
        0.5 * (1.0 + lax.erf(before * ROOT_HALF))
        + before * jnp.exp(-0.5 * before * before) * DENSITY
    )
    before_grad = (activated_grad * slope).astype(BF16)
    grad_bias_in = jnp.sum(before_grad.astype(F32), 0)
    grad_weight_in = lax.dot_general(
        normed_low, before_grad, (((0,), (0,)), ((), ())), preferred_element_type=F32
    ).astype(BF16)
    normed_grad = lax.dot_general(
        before_grad, weight_in, (((1,), (1,)), ((), ())), preferred_element_type=F32
    )
    small_grad = jnp.concatenate(
        [
            grad_bias_in.reshape(-1, C),
            grad_bias_out[None],
            grad_scale[None],
            jnp.zeros((SMALL - 6, C), F32),
        ]
    ).astype(BF16)
    return small_grad, grad_weight_in, grad_weight_out, normed_grad.reshape(normed.shape)


def adam_update(gradient, weights, first, second_moment):
    first_new = BETA_ONE * first + (1.0 - BETA_ONE) * gradient
    second_new = BETA_TWO * second_moment + (1.0 - BETA_TWO) * gradient * gradient
    update = first_new / FIRST_FIX / (jnp.sqrt(second_new / SECOND_FIX) + 1e-08)
    weights_new = weights * (1.0 - LEARNING * DECAY) - LEARNING * update
    return (weights_new, first_new, second_new)


def device_step(images_in, cotangent, master, moment, second, owner, offset):
    owners = lax.axis_size("fsdp")
    replicas = lax.axis_size("dp")
    me = lax.axis_index("fsdp")
    core = lax.axis_index("dp")
    bucket = master.shape[0]
    total_rows = owner.shape[0]
    rows = -(-bucket // (replicas * CHUNK)) * CHUNK

    ids = jnp.arange(owners, dtype=jnp.int32)
    positions = jnp.arange(total_rows, dtype=jnp.int32)
    begins = jnp.where(offset == 0, positions, 0)
    starts = jnp.sum(jnp.where(owner[None, :] == ids[:, None], begins[None, :], 0), 1)
    rank = jnp.sum((starts[None, :] < starts[:, None]).astype(jnp.int32), 1)
    later = jnp.where(starts[None, :] > starts[:, None], starts[None, :], total_rows)
    counts = jnp.min(later, 1) - starts
    chosen = rank[None, :] == ids[:, None]
    pick = lambda mask, values: jnp.sum(jnp.where(mask, values[None, :], 0), 1)

    mine_start = jnp.sum(jnp.where(ids == me, starts, 0))
    mine_count = jnp.sum(jnp.where(ids == me, counts, 0))
    head_shift = jnp.minimum(mine_start, IN_AT)

    lowered = jnp.pad(master, ((0, replicas * rows - bucket), (0, 0))).astype(BF16)
    mine = lax.dynamic_slice_in_dim(lowered, core * rows, rows, 0)
    head_from = jnp.concatenate([jnp.zeros((IN_AT, LANES), BF16), lowered[:IN_AT]])
    head_mine = lax.dynamic_slice_in_dim(head_from, IN_AT - head_shift, IN_AT, 0)
    held = jnp.arange(IN_AT)[:, None] < mine_start + mine_count
    head = sum_small(jnp.where(held, head_mine, jnp.zeros_like(head_mine)), owners)
    head = jnp.pad(head.astype(F32).reshape(HEAD, C), ((0, HEAD_PAD - HEAD), (0, 0)))

    widen = lambda value: jnp.pad(value[0], ((0, 0), (0, WIDE - SIDE), (0, 0)))
    image, cot_image = widen(images_in), widen(cotangent)
    normed, scaled, inverse = mix(image, head)

    gathered = lax.all_gather(mine, ("dp", "fsdp"), axis=0, tiled=True)
    small, weight_in, weight_out = unpack(
        gathered.reshape(replicas, owners * rows, LANES),
        pick(chosen, ids),
        pick(chosen, starts),
        pick(chosen, counts),
    )
    small_grad, grad_in, grad_out, normed_grad = forward_backward(
        normed, cot_image, small, weight_in, weight_out
    )

    if replicas == 2 and owners == 16:
        other = lambda value: lax.ppermute(value, "dp", [(0, 1), (1, 0)])
        far_out, far_in, far_small = other(grad_out), other(grad_in), other(small_grad)
        cross = rows * 9 // 64 // 32 * 32
        wide = -(-(rows - cross) // 4) // 16 * 16
        slim = (rows - cross) // 2 - wide
        groups = []
        at = 0
        for number, size in enumerate((wide, slim, wide, slim)):
            groups += [(number % 2, f, c, at, size) for f, c in ((8, 8), (4, 4), (0, 4))]
            at += size
        groups += [(2, 4 * k, 4, at, cross) for k in range(4)]
        spots = jnp.arange(16, dtype=jnp.int32)
        high, low, deep = spots >> 3, (spots >> 2) & 1, spots & 3
        tables = [deep * 4 + high * 2 + low, deep * 4 + low * 2 + high, spots]
        bases = jnp.concatenate(
            [pick((table ^ me)[:, None] == ids[None, :], starts) for table in tables]
        ) + core * rows
        packed = pack(
            bases, add(small_grad, far_small), (grad_in, far_in), (grad_out, far_out), owners, groups
        )
        normed_grad, packed = lax.optimization_barrier((normed_grad, packed))
        masks = [(2, 1), (1, 2)]
        home, *away = packed[12:]
        across = [swap(away[k - 1], 4 * k, owners) for k in (1, 2, 3)]
        sums, gates, behind = [], [], ()
        for chunk in range(2):
            firsts = []
            for k in range(2):
                far, near, kept = packed[6 * chunk + 3 * k : 6 * chunk + 3 * k + 3]
                far = after(far, behind) if behind else far
                firsts.append(first_phase(far, near, kept, masks[k], owners))
            behind = tuple(value[0] for value in firsts)
            seconds = [second_phase(*firsts[k], masks[k], owners) for k in range(2)]
            sums.append(last_phase(jnp.concatenate(seconds, 1), 4, owners))
            gates = [behind, tuple(seconds)]
        sums.append(last_phase(add(home, *across), 1, owners))
        half = jnp.concatenate(sums, 0)
        theirs = other(half)
        grad_low = jnp.where(
            core == 0, jnp.concatenate([half, theirs]), jnp.concatenate([theirs, half])
        )
    else:
        groups = [(0, 0, owners, part * rows, rows) for part in range(replicas)]
        packed = pack(starts, small_grad.astype(F32), (grad_in,), (grad_out,), owners, groups)
        stacked = jnp.concatenate([value.reshape(owners * rows, LANES) for value in packed])
        part = lax.psum_scatter(stacked, "dp", scatter_dimension=0, tiled=True)
        half = lax.psum_scatter(part, "fsdp", scatter_dimension=0, tiled=True)
        grad_low = lax.all_gather(half, "dp", axis=0, tiled=True)

    result, head_grad = unmix(image, cot_image, head, normed_grad, scaled, inverse)
    input_grad = result[None, :, :SIDE]
    head_low = head_grad[:HEAD].astype(BF16).reshape(IN_AT, LANES)
    head_low = add(head_low, *replica_others(head_low, replicas)).astype(BF16)
    if replicas == 2 and owners == 16:
        for shift, gate in zip((1, 4), gates, strict=True):
            head_low = after(head_low, gate)
            head_low = add(head_low, *[swap(head_low, k * shift, owners) for k in (1, 2, 3)]).astype(BF16)
    else:
        head_low = sum_small(head_low, owners)
    head_to = jnp.concatenate([head_low, jnp.zeros((IN_AT, LANES), BF16)])
    head_rows = lax.dynamic_slice_in_dim(head_to, head_shift, IN_AT, 0)
    slot = jnp.arange(bucket)[:, None]
    grad_low = jnp.where(
        slot < IN_AT - head_shift, jnp.pad(head_rows, ((0, bucket - IN_AT), (0, 0))), grad_low[:bucket]
    )
    grad_low = lax.optimization_barrier(grad_low)
    grad_full = jnp.where(slot < mine_count, grad_low.astype(F32), 0.0)
    new_master, new_moment, new_second = adam_update(grad_full, master, moment, second)
    return (input_grad, new_master, new_moment, new_second)


def solution(mesh):
    placed = (
        P(("dp", "fsdp"), None, None, None),
        P(("dp", "fsdp"), None, None, None),
        P("fsdp", None),
        P("fsdp", None),
        P("fsdp", None),
        P(),
        P(),
    )
    return jax.shard_map(
        device_step,
        mesh=mesh,
        in_specs=placed,
        out_specs=(
            P(("dp", "fsdp"), None, None, None),
            P("fsdp", None),
            P("fsdp", None),
            P("fsdp", None),
        ),
        check_vma=False,
    )
```
